32 devices in a mesh: groups: 2 (over y), row: 4 (over z), col: 4 (over x, core).
Axes of the slice: x: 2, y: 2, z: 4, core: 2. Of those that a mesh axis runs over, the one named last changes fastest.
Arguments:
- factor_blocks: bfloat16 [20, 4096, 4096], P('groups', 'row', 'col'), parts along dimension 0, may hold values from -0.0390625 to 0.0390625
- inverse_blocks: bfloat16 [10, 4096, 4096], P('groups', 'col', 'row'), parts along dimension 0, as said below
- right_sides: bfloat16 [10, 4096, 256], P('groups', 'row'), parts along dimension 0, may hold values from -6 to 6
Outputs:
- solution: bfloat16 [10, 4096, 256], P('groups', 'col', 'row'), parts along dimension 0
The draws below stay inside these ranges and needn't reach their ends.
There are 2 independent parts, one for each index of `groups`. The reference program is written for one: setup_inputs(seed, part) draws one part's arguments, and reference() takes and returns one part's arrays. A program takes and returns all parts, laid end to end along the dimension named above; each array names one. Nothing has to cross between parts.
Inputs may be any that keep to these rules, and one draw needn't show every extreme that they name: `inverse_blocks`: each block is lower triangular with a diagonal of 0.5 to 2, hence invertible.
All inputs are finite; a program needn't handle non-finite values.
Results may differ from the reference program's by a relative error of at most 0.0095.
Values may be sent and summed in bfloat16 or wider, within the bound.
A program may use at most 64 MiB of HBM per device.

```python
import jax
import jax.numpy as jnp
from jax import lax

BS = 4096
NB = 5
R = 256
ORDER = 20480
NPAIR = 10
N_ROW = 4


def draw_inverse_blocks(key, part):
    base = jax.random.fold_in(key, 4177)
    key_diag, key_off = jax.random.split(base, 2)
    diagonal = jnp.exp(jax.random.uniform(key_diag, (NB, BS), jnp.float32, jnp.log(0.5), jnp.log(2.0)))
    lower = jax.random.normal(key_off, (NB, BS, BS), jnp.float32) * (0.6 / jnp.sqrt(BS * 1.0))
    rows = jnp.arange(BS)[:, None]
    cols = jnp.arange(BS)[None, :]
    strict = (rows > cols).astype(jnp.float32)
    eye = (rows == cols).astype(jnp.float32)
    whole = diagonal[:, :, None] * eye[None] + lower * strict[None]
    return whole.astype(jnp.bfloat16)


def block_levels(stream_key, extent, shards, smallest, largest):
    def one(position, parts):
        draws = jax.random.uniform(jax.random.fold_in(jax.random.fold_in(stream_key, 6), position), (parts,), jnp.float32, smallest / len(shards), largest / len(shards))
        return jnp.repeat(jnp.exp(draws), extent[position] // parts).reshape((-1,) + (1,) * (len(extent) - position - 1))

    level = one(*shards[0])
    for cut in shards[1:]:
        level = level * one(*cut)
    return level


def normal_values(rng, dims, scale, reach, cuts=(), kind=jnp.bfloat16):
    result = jax.random.normal(rng, dims, jnp.float32) * scale
    if len(cuts) > 0:
        result = block_levels(rng, dims, cuts, -0.22, 0.18) * result
    return jnp.clip(result, min=-reach, max=reach).astype(kind)


def setup_inputs(seed: int = 0, part: int = 0) -> dict:
    seeds = jax.random.split(jax.random.key(seed), 4)
    part_splits = jax.random.split(jax.random.fold_in(seeds[3], part), 4)
    return {
        "factor_blocks": normal_values(part_splits[0], (NPAIR, BS, BS), ORDER ** -0.5, 0.0390625, ((1, 4), (2, 4))),
        "inverse_blocks": draw_inverse_blocks(jax.random.fold_in(jax.random.fold_in(seeds[3], part), 71), part),
        "right_sides": normal_values(part_splits[2], (NB, BS, R), 1.0, 6.0, ((1, 4),)),
    }


def pair_index(block_row, column_index):
    return block_row * (block_row - 1) // 2 + column_index


def reference(factor_blocks, inverse_blocks, right_sides):
    solved = []
    group_rows = BS // N_ROW
    for block_row in range(NB):
        residual = right_sides[block_row].astype(jnp.float32)
        if block_row > 0:
            strip = jnp.concatenate([factor_blocks[pair_index(block_row, j)] for j in range(block_row)], axis=1)
            known = jnp.concatenate(solved, axis=0)
            residual = residual - jnp.dot(strip, known, preferred_element_type=jnp.float32)
        residual_bf = residual.astype(jnp.bfloat16)
        inverse = inverse_blocks[block_row].astype(jnp.float32).reshape(BS, N_ROW, group_rows)
        grouped = residual_bf.astype(jnp.float32).reshape(N_ROW, group_rows, R)
        terms = jnp.einsum("iqk,qkr->qir", inverse, grouped, precision=lax.Precision.HIGHEST)
        solved.append(jnp.sum(terms, axis=0).astype(jnp.bfloat16))
    return jnp.stack(solved, axis=0)
```

```python
import functools

import jax
import jax.numpy as jnp
from jax import lax
from jax.experimental import pallas as pl
from jax.experimental.pallas import tpu as pltpu
from jax.sharding import PartitionSpec as P

MESH = pl.DeviceIdType.MESH
CHAINS = 2
PIECES = 4


def pair_index(block_row, column_index):
    return block_row * (block_row - 1) // 2 + column_index


def kernel(
    factor_hbm, inverse_hbm, right_hbm, solved,
    factor, inverse, right, partial, pair_out, pair_in, far_out, far_in, residual, line_out, line_in, cross_in,
    load_sem, col_send, col_recv, row_send, row_recv,
):
    f32, bf16 = jnp.float32, jnp.bfloat16
    steps, chains, col_rows, width = solved.shape
    rows = right.shape[1]
    half = rows // 2
    piece = col_rows // PIECES
    row_at = lax.axis_index("row")
    col_at = lax.axis_index("col")
    group_at = lax.axis_index("groups")
    core = lax.rem(col_at, 2)
    inner = jnp.logical_or(row_at == 1, row_at == 2)
    outer = jnp.logical_not(inner)

    sibling = (group_at, row_at, col_at + 1 - 2 * core)
    far = (group_at, row_at, lax.rem(col_at + 2, 4))
    beside = (group_at, row_at + 1 - 2 * lax.rem(row_at, 2), col_at)
    across = (group_at, 3 - row_at, col_at)

    loads = {}
    order = [("r", i) for i in range(steps)][:1] + [("i", 0)]
    for i in range(1, steps):
        order += [("r", i)] + [("f", pair_index(i, j)) for j in range(i)] + [("i", i)]
    sources = {"f": (factor_hbm, factor), "i": (inverse_hbm, inverse), "r": (right_hbm, right)}
    for slot, (kind, at) in enumerate(order):
        src, dst = sources[kind]
        loads[kind, at] = pltpu.make_async_copy(src.at[at], dst.at[at], load_sem.at[slot])
        loads[kind, at].start()
    waited = set()

    def loaded(kind, at):
        if (kind, at) not in waited:
            waited.add((kind, at))
            loads[kind, at].wait()

    barrier = pltpu.get_barrier_semaphore()
    for peer in (sibling, far, beside):
        pl.semaphore_signal(barrier, inc=1, device_id=peer, device_id_type=MESH)

    @pl.when(inner)
    def _():
        pl.semaphore_signal(barrier, inc=1, device_id=across, device_id_type=MESH)
        pl.semaphore_wait(barrier, 4)

    @pl.when(outer)
    def _():
        pl.semaphore_wait(barrier, 3)

    def remote(src, dst, send, recv, peer):
        return pltpu.make_async_remote_copy(
            src_ref=src, dst_ref=dst, send_sem=send, recv_sem=recv, device_id=peer, device_id_type=MESH
        )

    mine = pl.ds(pl.multiple_of(core * half, half), half)
    other = pl.ds(pl.multiple_of((1 - core) * half, half), half)

    def dot(a, b):
        return jnp.dot(a, b, preferred_element_type=f32)

    def chain(a):
        lanes = slice(a * width, (a + 1) * width)
        for i in range(steps):
            if i > 0:
                to_pair = remote(pair_out.at[i - 1, a], pair_in.at[i - 1, a], col_send.at[i - 1, a, 0], col_recv.at[i - 1, a, 0], sibling)
                to_far = remote(far_out.at[i - 1, a], far_in.at[i - 1, a], col_send.at[i - 1, a, 1], col_recv.at[i - 1, a, 1], far)
                back = remote(residual.at[i, a, mine], residual.at[i, a, mine], col_send.at[i - 1, a, 2], col_recv.at[i - 1, a, 2], sibling)
                at = pair_index(i, i - 1)
                loaded("f", at)
                value = dot(factor[at, other, :], solved[i - 1, a])
                if i > 1:
                    value = value + partial[a, other, :]
                pair_out[i - 1, a] = value.astype(bf16)
                to_pair.start()
                value = dot(factor[at, mine, :], solved[i - 1, a])
                if i > 1:
                    value = value + partial[a, mine, :]
                partial[a, mine, :] = value
                yield
                to_pair.wait_recv()
                far_out[i - 1, a] = (partial[a, mine, :] + pair_in[i - 1, a].astype(f32)).astype(bf16)
                to_far.start()
                yield
                to_far.wait_recv()
                loaded("r", i)
                total = far_out[i - 1, a].astype(f32) + far_in[i - 1, a].astype(f32)
                residual[i, a, mine, :] = (right[i, mine, lanes].astype(f32) - total).astype(bf16)
                back.start()
                yield
                back.wait_recv()
            else:
                loaded("r", 0)
                residual[0, a] = right[0, :, lanes]
            loaded("i", i)
            spans = [pl.ds(k * piece, piece) for k in range(PIECES)]
            first = [remote(line_out.at[i, a, s], line_in.at[i, a, s], row_send.at[i, a, 0, k], row_recv.at[i, a, 0, k], beside) for k, s in enumerate(spans)]
            cross = [remote(line_out.at[i, a, s], cross_in.at[i, a, s], row_send.at[i, a, 1, k], row_recv.at[i, a, 1, k], across) for k, s in enumerate(spans)]
            last = [remote(solved.at[i, a, s], solved.at[i, a, s], row_send.at[i, a, 2, k], row_recv.at[i, a, 2, k], beside) for k, s in enumerate(spans)]
            for k, s in enumerate(spans):
                term = dot(inverse[i, s, :], residual[i, a])

                @pl.when(outer)
                def _():
                    line_out[i, a, s, :] = term.astype(bf16)
                    first[k].start()

                @pl.when(inner)
                def _():
                    first[k].wait_recv()
                    line_out[i, a, s, :] = (term + line_in[i, a, s, :].astype(f32)).astype(bf16)
                    cross[k].start()

            if i > 0 and i + 1 < steps:
                for j in range(i):
                    loaded("f", pair_index(i + 1, j))

                def ahead(t, carry):
                    tile = pl.ds(pl.multiple_of(t * piece, piece), piece)
                    value = dot(factor[pair_index(i + 1, 0), tile, :], solved[0, a])
                    for j in range(1, i):
                        value = value + dot(factor[pair_index(i + 1, j), tile, :], solved[j, a])
                    partial[a, tile, :] = value
                    return carry

                lax.fori_loop(0, rows // piece, ahead, 0)
            yield

            @pl.when(inner)
            def _():
                for k, s in enumerate(spans):
                    cross[k].wait_recv()
                    value = line_out[i, a, s, :].astype(f32) + cross_in[i, a, s, :].astype(f32)
                    solved[i, a, s, :] = value.astype(bf16)
                    last[k].start()

            yield

            @pl.when(outer)
            def _():
                for k in range(PIECES):
                    last[k].wait_recv()
                    first[k].wait_send()

            @pl.when(inner)
            def _():
                for k in range(PIECES):
                    cross[k].wait_send()
                    last[k].wait_send()

            if i > 0:
                to_pair.wait_send()
                to_far.wait_send()
                back.wait_send()

    running = [chain(a) for a in range(chains)]
    turn = 0
    while running:
        active = [g for a, g in enumerate(running) if a * 3 <= turn]
        for g in active:
            try:
                next(g)
            except StopIteration:
                running = [other_g for other_g in running if other_g is not g]
        turn += 1


def line_solve(factor_blocks, inverse_blocks, right_sides):
    steps, rows, angles = right_sides.shape
    pairs = factor_blocks.shape[0]
    col_rows = inverse_blocks.shape[1]
    width = angles // CHAINS
    half = rows // 2
    bf16 = jnp.bfloat16
    sweeps = steps - 1
    wide = (steps, CHAINS, col_rows, width)
    dma = pltpu.SemaphoreType.DMA
    solved = pl.pallas_call(
        kernel,
        out_shape=jax.ShapeDtypeStruct(wide, bf16),
        in_specs=[pl.BlockSpec(memory_space=pl.ANY)] * 3,
        out_specs=pl.BlockSpec(memory_space=pltpu.VMEM),
        scratch_shapes=[
            pltpu.VMEM(factor_blocks.shape, bf16),
            pltpu.VMEM(inverse_blocks.shape, bf16),
            pltpu.VMEM(right_sides.shape, bf16),
            pltpu.VMEM((CHAINS, rows, width), jnp.float32),
            pltpu.VMEM((sweeps, CHAINS, half, width), bf16),
            pltpu.VMEM((sweeps, CHAINS, half, width), bf16),
            pltpu.VMEM((sweeps, CHAINS, half, width), bf16),
            pltpu.VMEM((sweeps, CHAINS, half, width), bf16),
            pltpu.VMEM((steps, CHAINS, rows, width), bf16),
            pltpu.VMEM(wide, bf16),
            pltpu.VMEM(wide, bf16),
            pltpu.VMEM(wide, bf16),
            dma((pairs + 2 * steps,)),
            dma((sweeps, CHAINS, 3)),
            dma((sweeps, CHAINS, 3)),
            dma((steps, CHAINS, 3, PIECES)),
            dma((steps, CHAINS, 3, PIECES)),
        ],
        compiler_params=pltpu.CompilerParams(
            collective_id=0, has_side_effects=True, vmem_limit_bytes=67043328
        ),
    )(factor_blocks, inverse_blocks, right_sides)
    share = angles // lax.axis_size("row")
    start = lax.axis_index("row") * share
    held = lax.dynamic_index_in_dim(solved, start // width, axis=1, keepdims=False)
    return lax.dynamic_slice_in_dim(held, lax.rem(start, width), share, axis=2)


def plain_solve(factor_blocks, inverse_blocks, right_sides):
    steps_total = right_sides.shape[0]
    solved = []
    outputs = []
    for block_row in range(steps_total):
        residual = right_sides[block_row].astype(jnp.float32)
        if block_row > 0:
            partial_value = jnp.zeros(residual.shape, jnp.float32)
            for column_index in range(block_row):
                partial_value = partial_value + jnp.dot(
                    factor_blocks[pair_index(block_row, column_index)],
                    solved[column_index],
                    preferred_element_type=jnp.float32,
                )
            residual = residual - lax.psum(partial_value, "col")
        residual_bf = residual.astype(jnp.bfloat16)
        term = jnp.dot(inverse_blocks[block_row], residual_bf, preferred_element_type=jnp.float32)
        share = lax.psum_scatter(term, "row", scatter_dimension=1, tiled=True).astype(jnp.bfloat16)
        outputs.append(share)
        if block_row + 1 < steps_total:
            solved.append(lax.all_gather(share, "row", axis=1, tiled=True))
    return jnp.stack(outputs, axis=0)


def solution(mesh):
    placed = (P("groups", "row", "col"), P("groups", "col", "row"), P("groups", "row", None))
    per_device = line_solve if mesh.shape["row"] == 4 and mesh.shape["col"] == 4 else plain_solve
    return jax.shard_map(
        per_device, mesh=mesh, in_specs=placed, out_specs=P("groups", "col", "row"), check_vma=False
    )
```

```python
import functools

import jax
import jax.numpy as jnp
from jax import lax
from jax.experimental import pallas as pl
from jax.experimental.pallas import tpu as pltpu
from jax.sharding import PartitionSpec as P

MESH = pl.DeviceIdType.MESH
CHAINS = 2
PIECES = 4
STAGGER = 1


def pair_index(block_row, column_index):
    return block_row * (block_row - 1) // 2 + column_index


def kernel(
    factor_hbm, inverse_hbm, right_hbm, solved,
    factor, inverse, right, partial, pair_out, pair_in, far_out, far_in, residual, line_out, line_in, cross_in,
    load_sem, col_send, col_recv, row_send, row_recv,
):
    f32, bf16 = jnp.float32, jnp.bfloat16
    steps, chains, col_rows, width = solved.shape
    rows = right.shape[1]
    half = rows // 2
    piece = col_rows // PIECES
    row_at = lax.axis_index("row")
    col_at = lax.axis_index("col")
    group_at = lax.axis_index("groups")
    core = lax.rem(col_at, 2)
    inner = jnp.logical_or(row_at == 1, row_at == 2)
    outer = jnp.logical_not(inner)
    owns = [row_at * chains // 4 == a for a in range(chains)]

    sibling = (group_at, row_at, col_at + 1 - 2 * core)
    far = (group_at, row_at, lax.rem(col_at + 2, 4))
    beside = (group_at, row_at + 1 - 2 * lax.rem(row_at, 2), col_at)
    across = (group_at, 3 - row_at, col_at)

    loads = {}
    order = [("r", i) for i in range(steps)][:1] + [("i", 0)]
    for i in range(1, steps):
        order += [("r", i)] + [("f", pair_index(i, j)) for j in range(i)] + [("i", i)]
    sources = {"f": (factor_hbm, factor), "i": (inverse_hbm, inverse), "r": (right_hbm, right)}
    for slot, (kind, at) in enumerate(order):
        src, dst = sources[kind]
        loads[kind, at] = pltpu.make_async_copy(src.at[at], dst.at[at], load_sem.at[slot])
        loads[kind, at].start()
    waited = set()

    def loaded(kind, at):
        if (kind, at) not in waited:
            waited.add((kind, at))
            loads[kind, at].wait()

    barrier = pltpu.get_barrier_semaphore()
    for peer in (sibling, far, beside):
        pl.semaphore_signal(barrier, inc=1, device_id=peer, device_id_type=MESH)

    @pl.when(inner)
    def _():
        pl.semaphore_signal(barrier, inc=1, device_id=across, device_id_type=MESH)
        pl.semaphore_wait(barrier, 4)

    @pl.when(outer)
    def _():
        pl.semaphore_wait(barrier, 3)

    def remote(src, dst, send, recv, peer):
        return pltpu.make_async_remote_copy(
            src_ref=src, dst_ref=dst, send_sem=send, recv_sem=recv, device_id=peer, device_id_type=MESH
        )

    mine = pl.ds(pl.multiple_of(core * half, half), half)
    other = pl.ds(pl.multiple_of((1 - core) * half, half), half)

    def dot(a, b):
        return jnp.dot(a, b, preferred_element_type=f32)

    def chain(a):
        lanes = slice(a * width, (a + 1) * width)
        for i in range(steps):
            if i > 0:
                to_pair = remote(pair_out.at[i - 1, a], pair_in.at[i - 1, a], col_send.at[i - 1, a, 0], col_recv.at[i - 1, a, 0], sibling)
                to_far = remote(far_out.at[i - 1, a], far_in.at[i - 1, a], col_send.at[i - 1, a, 1], col_recv.at[i - 1, a, 1], far)
                back = remote(residual.at[i, a, mine], residual.at[i, a, mine], col_send.at[i - 1, a, 2], col_recv.at[i - 1, a, 2], sibling)
                at = pair_index(i, i - 1)
                loaded("f", at)
                value = dot(factor[at, other, :], solved[i - 1, a])
                if i > 1:
                    value = value + partial[a, other, :]
                pair_out[i - 1, a] = value.astype(bf16)
                to_pair.start()
                value = dot(factor[at, mine, :], solved[i - 1, a])
                if i > 1:
                    value = value + partial[a, mine, :]
                partial[a, mine, :] = value
                yield
                to_pair.wait_recv()
                far_out[i - 1, a] = (partial[a, mine, :] + pair_in[i - 1, a].astype(f32)).astype(bf16)
                to_far.start()
                yield
                to_far.wait_recv()
                loaded("r", i)
                total = far_out[i - 1, a].astype(f32) + far_in[i - 1, a].astype(f32)
                residual[i, a, mine, :] = (right[i, mine, lanes].astype(f32) - total).astype(bf16)
                back.start()
                yield
                back.wait_recv()
            else:
                loaded("r", 0)
                residual[0, a] = right[0, :, lanes]
            loaded("i", i)
            final = i + 1 == steps
            takes = owns[a] if final else True
            gives = jnp.logical_not(owns[a]) if final else True
            spans = [pl.ds(k * piece, piece) for k in range(PIECES)]
            first = [remote(line_out.at[i, a, s], line_in.at[i, a, s], row_send.at[i, a, 0, k], row_recv.at[i, a, 0, k], beside) for k, s in enumerate(spans)]
            cross = [remote(line_out.at[i, a, s], cross_in.at[i, a, s], row_send.at[i, a, 1, k], row_recv.at[i, a, 1, k], across) for k, s in enumerate(spans)]
            last = [remote(solved.at[i, a, s], solved.at[i, a, s], row_send.at[i, a, 2, k], row_recv.at[i, a, 2, k], beside) for k, s in enumerate(spans)]
            for k, s in enumerate(spans):
                term = dot(inverse[i, s, :], residual[i, a])

                @pl.when(outer)
                def _():
                    line_out[i, a, s, :] = term.astype(bf16)
                    first[k].start()

                @pl.when(inner)
                def _():
                    first[k].wait_recv()
                    line_out[i, a, s, :] = (term + line_in[i, a, s, :].astype(f32)).astype(bf16)

                @pl.when(jnp.logical_and(inner, gives))
                def _():
                    cross[k].start()

            if i > 0 and i + 1 < steps:
                for j in range(i):
                    loaded("f", pair_index(i + 1, j))

                def ahead(t, carry):
                    tile = pl.ds(pl.multiple_of(t * piece, piece), piece)
                    value = dot(factor[pair_index(i + 1, 0), tile, :], solved[0, a])
                    for j in range(1, i):
                        value = value + dot(factor[pair_index(i + 1, j), tile, :], solved[j, a])
                    partial[a, tile, :] = value
                    return carry

                lax.fori_loop(0, rows // piece, ahead, 0)
            yield

            @pl.when(jnp.logical_and(inner, takes))
            def _():
                for k, s in enumerate(spans):
                    cross[k].wait_recv()
                    value = line_out[i, a, s, :].astype(f32) + cross_in[i, a, s, :].astype(f32)
                    solved[i, a, s, :] = value.astype(bf16)
                    last[k].start()

            yield

            @pl.when(jnp.logical_and(outer, takes))
            def _():
                for k in range(PIECES):
                    last[k].wait_recv()

            @pl.when(outer)
            def _():
                for k in range(PIECES):
                    first[k].wait_send()

            @pl.when(jnp.logical_and(inner, gives))
            def _():
                for k in range(PIECES):
                    cross[k].wait_send()

            @pl.when(jnp.logical_and(inner, takes))
            def _():
                for k in range(PIECES):
                    last[k].wait_send()

            if i > 0:
                to_pair.wait_send()
                to_far.wait_send()
                back.wait_send()

    running = [chain(a) for a in range(chains)]
    turn = 0
    while running:
        active = [g for a, g in enumerate(running) if a * STAGGER <= turn]
        for g in active:
            try:
                next(g)
            except StopIteration:
                running = [other_g for other_g in running if other_g is not g]
        turn += 1


def line_solve(factor_blocks, inverse_blocks, right_sides):
    steps, rows, angles = right_sides.shape
    pairs = factor_blocks.shape[0]
    col_rows = inverse_blocks.shape[1]
    width = angles // CHAINS
    half = rows // 2
    bf16 = jnp.bfloat16
    sweeps = steps - 1
    wide = (steps, CHAINS, col_rows, width)
    dma = pltpu.SemaphoreType.DMA
    solved = pl.pallas_call(
        kernel,
        out_shape=jax.ShapeDtypeStruct(wide, bf16),
        in_specs=[pl.BlockSpec(memory_space=pl.ANY)] * 3,
        out_specs=pl.BlockSpec(memory_space=pltpu.VMEM),
        scratch_shapes=[
            pltpu.VMEM(factor_blocks.shape, bf16),
            pltpu.VMEM(inverse_blocks.shape, bf16),
            pltpu.VMEM(right_sides.shape, bf16),
            pltpu.VMEM((CHAINS, rows, width), jnp.float32),
            pltpu.VMEM((sweeps, CHAINS, half, width), bf16),
            pltpu.VMEM((sweeps, CHAINS, half, width), bf16),
            pltpu.VMEM((sweeps, CHAINS, half, width), bf16),
            pltpu.VMEM((sweeps, CHAINS, half, width), bf16),
            pltpu.VMEM((steps, CHAINS, rows, width), bf16),
            pltpu.VMEM(wide, bf16),
            pltpu.VMEM(wide, bf16),
            pltpu.VMEM(wide, bf16),
            dma((pairs + 2 * steps,)),
            dma((sweeps, CHAINS, 3)),
            dma((sweeps, CHAINS, 3)),
            dma((steps, CHAINS, 3, PIECES)),
            dma((steps, CHAINS, 3, PIECES)),
        ],
        compiler_params=pltpu.CompilerParams(
            collective_id=0, has_side_effects=True, vmem_limit_bytes=67043328
        ),
    )(factor_blocks, inverse_blocks, right_sides)
    share = angles // lax.axis_size("row")
    start = lax.axis_index("row") * share
    held = lax.dynamic_index_in_dim(solved, start // width, axis=1, keepdims=False)
    return lax.dynamic_slice_in_dim(held, lax.rem(start, width), share, axis=2)


def plain_solve(factor_blocks, inverse_blocks, right_sides):
    steps_total = right_sides.shape[0]
    solved = []
    outputs = []
    for block_row in range(steps_total):
        residual = right_sides[block_row].astype(jnp.float32)
        if block_row > 0:
            partial_value = jnp.zeros(residual.shape, jnp.float32)
            for column_index in range(block_row):
                partial_value = partial_value + jnp.dot(
                    factor_blocks[pair_index(block_row, column_index)],
                    solved[column_index],
                    preferred_element_type=jnp.float32,
                )
            residual = residual - lax.psum(partial_value, "col")
        residual_bf = residual.astype(jnp.bfloat16)
        term = jnp.dot(inverse_blocks[block_row], residual_bf, preferred_element_type=jnp.float32)
        share = lax.psum_scatter(term, "row", scatter_dimension=1, tiled=True).astype(jnp.bfloat16)
        outputs.append(share)
        if block_row + 1 < steps_total:
            solved.append(lax.all_gather(share, "row", axis=1, tiled=True))
    return jnp.stack(outputs, axis=0)


def solution(mesh):
    placed = (P("groups", "row", "col"), P("groups", "col", "row"), P("groups", "row", None))
    per_device = line_solve if mesh.shape["row"] == 4 and mesh.shape["col"] == 4 else plain_solve
    return jax.shard_map(
        per_device, mesh=mesh, in_specs=placed, out_specs=P("groups", "col", "row"), check_vma=False
    )
```

```python
import functools

import jax
import jax.numpy as jnp
from jax import lax
from jax.experimental import pallas as pl
from jax.experimental.pallas import tpu as pltpu
from jax.sharding import PartitionSpec as P

MESH = pl.DeviceIdType.MESH
CHAINS = 2
PIECES = 4
STAGGER = 1


def pair_index(block_row, column_index):
    return block_row * (block_row - 1) // 2 + column_index


def kernel(
    factor_hbm, inverse_hbm, right_hbm, solved,
    factor, inverse, right, partial, pair_out, pair_in, far_out, far_in, residual, line_out, line_in, cross_in,
    load_sem, col_send, col_recv, row_send, row_recv,
):
    f32, bf16 = jnp.float32, jnp.bfloat16
    steps, chains, col_rows, width = solved.shape
    rows = right.shape[1]
    half = rows // 2
    piece = col_rows // PIECES
    row_at = lax.axis_index("row")
    col_at = lax.axis_index("col")
    group_at = lax.axis_index("groups")
    core = lax.rem(col_at, 2)
    inner = jnp.logical_or(row_at == 1, row_at == 2)
    outer = jnp.logical_not(inner)
    owns = [row_at * chains // 4 == a for a in range(chains)]

    sibling = (group_at, row_at, col_at + 1 - 2 * core)
    far = (group_at, row_at, lax.rem(col_at + 2, 4))
    beside = (group_at, row_at + 1 - 2 * lax.rem(row_at, 2), col_at)
    across = (group_at, 3 - row_at, col_at)

    loads = {}
    order = [("r", i) for i in range(steps)][:1] + [("i", 0)]
    for i in range(1, steps):
        order += [("r", i)] + [("f", pair_index(i, j)) for j in range(i)] + [("i", i)]
    sources = {"f": (factor_hbm, factor), "i": (inverse_hbm, inverse), "r": (right_hbm, right)}
    for slot, (kind, at) in enumerate(order):
        src, dst = sources[kind]
        loads[kind, at] = pltpu.make_async_copy(src.at[at], dst.at[at], load_sem.at[slot])
        loads[kind, at].start()
    waited = set()

    def loaded(kind, at):
        if (kind, at) not in waited:
            waited.add((kind, at))
            loads[kind, at].wait()

    barrier = pltpu.get_barrier_semaphore()
    for peer in (sibling, far, beside):
        pl.semaphore_signal(barrier, inc=1, device_id=peer, device_id_type=MESH)

    @pl.when(inner)
    def _():
        pl.semaphore_signal(barrier, inc=1, device_id=across, device_id_type=MESH)
        pl.semaphore_wait(barrier, 4)

    @pl.when(outer)
    def _():
        pl.semaphore_wait(barrier, 3)

    def remote(src, dst, send, recv, peer):
        return pltpu.make_async_remote_copy(
            src_ref=src, dst_ref=dst, send_sem=send, recv_sem=recv, device_id=peer, device_id_type=MESH
        )

    mine = pl.ds(pl.multiple_of(core * half, half), half)
    other = pl.ds(pl.multiple_of((1 - core) * half, half), half)

    def dot(a, b):
        return jnp.dot(a, b, preferred_element_type=f32)

    def chain(a):
        lanes = slice(a * width, (a + 1) * width)
        for i in range(steps):
            if i > 0:
                to_pair = remote(pair_out.at[i - 1, a], pair_in.at[i - 1, a], col_send.at[i - 1, a, 0], col_recv.at[i - 1, a, 0], sibling)
                to_far = remote(far_out.at[i - 1, a], far_in.at[i - 1, a], col_send.at[i - 1, a, 1], col_recv.at[i - 1, a, 1], far)
                back = remote(residual.at[i, a, mine], residual.at[i, a, mine], col_send.at[i - 1, a, 2], col_recv.at[i - 1, a, 2], sibling)
                at = pair_index(i, i - 1)
                loaded("f", at)
                value = dot(factor[at, other, :], solved[i - 1, a])
                if i > 1:
                    value = value + partial[a, other, :]
                pair_out[i - 1, a] = value.astype(bf16)
                to_pair.start()
                value = dot(factor[at, mine, :], solved[i - 1, a])
                if i > 1:
                    value = value + partial[a, mine, :]
                partial[a, mine, :] = value
                yield
                to_pair.wait_recv()
                far_out[i - 1, a] = (partial[a, mine, :] + pair_in[i - 1, a].astype(f32)).astype(bf16)
                to_far.start()
                yield
                to_far.wait_recv()
                loaded("r", i)
                total = far_out[i - 1, a].astype(f32) + far_in[i - 1, a].astype(f32)
                residual[i, a, mine, :] = (right[i, mine, lanes].astype(f32) - total).astype(bf16)
                back.start()
                yield
                back.wait_recv()
            else:
                loaded("r", 0)
                residual[0, a] = right[0, :, lanes]
            loaded("i", i)
            final = i + 1 == steps
            takes = owns[a] if final else True
            gives = jnp.logical_not(owns[a]) if final else True
            spans = [pl.ds(k * piece, piece) for k in range(PIECES)]
            first = [remote(line_out.at[i, a, s], line_in.at[i, a, s], row_send.at[i, a, 0, k], row_recv.at[i, a, 0, k], beside) for k, s in enumerate(spans)]
            cross = [remote(line_out.at[i, a, s], cross_in.at[i, a, s], row_send.at[i, a, 1, k], row_recv.at[i, a, 1, k], across) for k, s in enumerate(spans)]
            last = [remote(solved.at[i, a, s], solved.at[i, a, s], row_send.at[i, a, 2, k], row_recv.at[i, a, 2, k], beside) for k, s in enumerate(spans)]
            for k, s in enumerate(spans):
                term = dot(inverse[i, s, :], residual[i, a])

                @pl.when(outer)
                def _():
                    line_out[i, a, s, :] = term.astype(bf16)
                    first[k].start()

                @pl.when(inner)
                def _():
                    partial[a, s, :] = term

            yield

            for k, s in enumerate(spans):

                @pl.when(inner)
                def _():
                    first[k].wait_recv()
                    value = partial[a, s, :] + line_in[i, a, s, :].astype(f32)
                    line_out[i, a, s, :] = value.astype(bf16)

                @pl.when(jnp.logical_and(inner, gives))
                def _():
                    cross[k].start()

            if i > 0 and i + 1 < steps:
                for j in range(i):
                    loaded("f", pair_index(i + 1, j))

                def ahead(t, carry):
                    tile = pl.ds(pl.multiple_of(t * piece, piece), piece)
                    value = dot(factor[pair_index(i + 1, 0), tile, :], solved[0, a])
                    for j in range(1, i):
                        value = value + dot(factor[pair_index(i + 1, j), tile, :], solved[j, a])
                    partial[a, tile, :] = value
                    return carry

                lax.fori_loop(0, rows // piece, ahead, 0)
            yield

            @pl.when(jnp.logical_and(inner, takes))
            def _():
                for k, s in enumerate(spans):
                    cross[k].wait_recv()
                    value = line_out[i, a, s, :].astype(f32) + cross_in[i, a, s, :].astype(f32)
                    solved[i, a, s, :] = value.astype(bf16)
                    last[k].start()

            yield

            @pl.when(jnp.logical_and(outer, takes))
            def _():
                for k in range(PIECES):
                    last[k].wait_recv()

            @pl.when(outer)
            def _():
                for k in range(PIECES):
                    first[k].wait_send()

            @pl.when(jnp.logical_and(inner, gives))
            def _():
                for k in range(PIECES):
                    cross[k].wait_send()

            @pl.when(jnp.logical_and(inner, takes))
            def _():
                for k in range(PIECES):
                    last[k].wait_send()

            if i > 0:
                to_pair.wait_send()
                to_far.wait_send()
                back.wait_send()

    running = [chain(a) for a in range(chains)]
    turn = 0
    while running:
        active = [g for a, g in enumerate(running) if a * STAGGER <= turn]
        for g in active:
            try:
                next(g)
            except StopIteration:
                running = [other_g for other_g in running if other_g is not g]
        turn += 1


def line_solve(factor_blocks, inverse_blocks, right_sides):
    steps, rows, angles = right_sides.shape
    pairs = factor_blocks.shape[0]
    col_rows = inverse_blocks.shape[1]
    width = angles // CHAINS
    half = rows // 2
    bf16 = jnp.bfloat16
    sweeps = steps - 1
    wide = (steps, CHAINS, col_rows, width)
    dma = pltpu.SemaphoreType.DMA
    solved = pl.pallas_call(
        kernel,
        out_shape=jax.ShapeDtypeStruct(wide, bf16),
        in_specs=[pl.BlockSpec(memory_space=pl.ANY)] * 3,
        out_specs=pl.BlockSpec(memory_space=pltpu.VMEM),
        scratch_shapes=[
            pltpu.VMEM(factor_blocks.shape, bf16),
            pltpu.VMEM(inverse_blocks.shape, bf16),
            pltpu.VMEM(right_sides.shape, bf16),
            pltpu.VMEM((CHAINS, rows, width), jnp.float32),
            pltpu.VMEM((sweeps, CHAINS, half, width), bf16),
            pltpu.VMEM((sweeps, CHAINS, half, width), bf16),
            pltpu.VMEM((sweeps, CHAINS, half, width), bf16),
            pltpu.VMEM((sweeps, CHAINS, half, width), bf16),
            pltpu.VMEM((steps, CHAINS, rows, width), bf16),
            pltpu.VMEM(wide, bf16),
            pltpu.VMEM(wide, bf16),
            pltpu.VMEM(wide, bf16),
            dma((pairs + 2 * steps,)),
            dma((sweeps, CHAINS, 3)),
            dma((sweeps, CHAINS, 3)),
            dma((steps, CHAINS, 3, PIECES)),
            dma((steps, CHAINS, 3, PIECES)),
        ],
        compiler_params=pltpu.CompilerParams(
            collective_id=0, has_side_effects=True, vmem_limit_bytes=67043328
        ),
    )(factor_blocks, inverse_blocks, right_sides)
    share = angles // lax.axis_size("row")
    start = lax.axis_index("row") * share
    held = lax.dynamic_index_in_dim(solved, start // width, axis=1, keepdims=False)
    return lax.dynamic_slice_in_dim(held, lax.rem(start, width), share, axis=2)


def plain_solve(factor_blocks, inverse_blocks, right_sides):
    steps_total = right_sides.shape[0]
    solved = []
    outputs = []
    for block_row in range(steps_total):
        residual = right_sides[block_row].astype(jnp.float32)
        if block_row > 0:
            partial_value = jnp.zeros(residual.shape, jnp.float32)
            for column_index in range(block_row):
                partial_value = partial_value + jnp.dot(
                    factor_blocks[pair_index(block_row, column_index)],
                    solved[column_index],
                    preferred_element_type=jnp.float32,
                )
            residual = residual - lax.psum(partial_value, "col")
        residual_bf = residual.astype(jnp.bfloat16)
        term = jnp.dot(inverse_blocks[block_row], residual_bf, preferred_element_type=jnp.float32)
        share = lax.psum_scatter(term, "row", scatter_dimension=1, tiled=True).astype(jnp.bfloat16)
        outputs.append(share)
        if block_row + 1 < steps_total:
            solved.append(lax.all_gather(share, "row", axis=1, tiled=True))
    return jnp.stack(outputs, axis=0)


def solution(mesh):
    placed = (P("groups", "row", "col"), P("groups", "col", "row"), P("groups", "row", None))
    per_device = line_solve if mesh.shape["row"] == 4 and mesh.shape["col"] == 4 else plain_solve
    return jax.shard_map(
        per_device, mesh=mesh, in_specs=placed, out_specs=P("groups", "col", "row"), check_vma=False
    )
```
